32 devices in a mesh: runs: 1, cfg: 32 (over z, y, x, core).
Axes of the slice: x: 2, y: 2, z: 4, core: 2. Of those that a mesh axis runs over, the one named last changes fastest.
Arguments:
- amplitudes: float32 [2, 512, 128, 512], P('runs', 'cfg')
- prop_third: float32 [2, 512, 512], replicated
- bitmasks_first: int32 [512], replicated, may hold values from 0 to 10922, as said below
- bitmasks_second: int32 [128], replicated, may hold values from 0 to 10922, as said below
- bitmasks_third: int32 [512], P('cfg'), may hold values from 0 to 10922, as said below
- detune_steps: int32 [3], P('runs'), may hold values from 0 to 15
Outputs:
- density: float32 [512, 2, 512], P(('runs', 'cfg'))
The draws below stay inside these ranges and needn't reach their ends.
Inputs may be any that keep to these rules, and one draw needn't show every extreme that they name: `bitmasks_first`: 512 different numbers, none with two adjacent bits set. `bitmasks_second`: 128 different numbers, none with two adjacent bits set. `bitmasks_third`: 512 different numbers, none with two adjacent bits set.
All inputs are finite; a program needn't handle non-finite values.
Results may differ from the reference program's by a relative error of at most 0.00005.
Values sent between devices are 32-bit elements; how exact they have to be, the bound alone decides.
A program may use at most 64 MiB of HBM per device.

```python
import math
import jax
import jax.numpy as jnp
from jax import lax

NA = 512
NB = 128
NC = 512


factor_count = 16


def independent_sets(key, wanted):
    candidates = jnp.arange(16384, dtype=jnp.int32)
    valid = candidates & jnp.right_shift(candidates, 1) == 0
    scores = jax.random.randint(key, (16384,), 0, 16384, dtype=jnp.int32) * 16384 + candidates
    scores = jnp.where(valid, scores, 268435456 + candidates)
    order = jnp.argsort(scores, stable=True)
    return candidates[order[:wanted]]


def propagator(key, width):
    noise = jax.random.normal(key, (2, width, width), jnp.float32)
    noise = noise * (0.6 / math.sqrt(2.0 * width))
    identity = jnp.eye(width, dtype=jnp.float32)
    return noise + jnp.stack([identity, jnp.zeros_like(identity)])


def draw_amplitudes(key, part):
    keys = jax.random.split(jax.random.fold_in(key, 11), 3)
    left = jax.random.normal(keys[0], (2, NC * NB, factor_count), jnp.float32)
    right = jax.random.normal(keys[1], (2, factor_count, NA), jnp.float32)
    noise = jax.random.normal(keys[2], (2, NC * NB, NA), jnp.float32)
    low_real = jnp.dot(left[0], right[0]) - jnp.dot(left[1], right[1])
    low_imag = jnp.dot(left[0], right[1]) + jnp.dot(left[1], right[0])
    low = jnp.stack([low_real, low_imag]) / math.sqrt(2.0 * factor_count)
    full = (low + 0.5 * noise) / math.sqrt(1.0 * NC * NB)
    return full.reshape(2, NC, NB, NA)


def draw_prop_third(key, part):
    return propagator(jax.random.fold_in(key, 23), NC)


def draw_bitmasks_first(key, part):
    return independent_sets(jax.random.fold_in(key, 31), NA)


def draw_bitmasks_second(key, part):
    return independent_sets(jax.random.fold_in(key, 32), NB)


def draw_bitmasks_third(key, part):
    return independent_sets(jax.random.fold_in(key, 33), NC)


def setup_inputs(seed: int = 0, part: int = 0) -> dict:
    splits = jax.random.split(jax.random.key(seed), 7)
    part_keys = jax.random.split(jax.random.fold_in(splits[6], part), 7)
    return {
        "amplitudes": draw_amplitudes(jax.random.fold_in(jax.random.fold_in(splits[6], part), 71), part),
        "prop_third": draw_prop_third(jax.random.fold_in(splits[6], 71), part),
        "bitmasks_first": draw_bitmasks_first(jax.random.fold_in(splits[6], 71), part),
        "bitmasks_second": draw_bitmasks_second(jax.random.fold_in(splits[6], 71), part),
        "bitmasks_third": draw_bitmasks_third(jax.random.fold_in(splits[6], 71), part),
        "detune_steps": jax.random.randint(part_keys[5], (3,), 0, 16).astype(jnp.int32),
    }


angle_step = 0.2
pair_angle = 0.7
atom_count = 14


def atom_bit(bitmasks, which):
    return (jnp.right_shift(bitmasks, which) & 1).astype(jnp.float32)


def occupation(bitmasks):
    total = jnp.zeros(bitmasks.shape, jnp.float32)
    for which in range(atom_count):
        total = total + atom_bit(bitmasks, which)
    return total


def boundary_terms(first, second, third, detune_steps):
    scaled = detune_steps.astype(jnp.float32) * angle_step
    phase_first = scaled[0] * occupation(first)
    phase_second = scaled[1] * occupation(second)
    phase_third = scaled[2] * occupation(third)
    last_first = atom_bit(first, 13)[None, None, :]
    near_first = atom_bit(first, 12)[None, None, :]
    head_second = atom_bit(second, 0)[None, :, None]
    next_second = atom_bit(second, 1)[None, :, None]
    last_second = atom_bit(second, 13)[None, :, None]
    near_second = atom_bit(second, 12)[None, :, None]
    head_third = atom_bit(third, 0)[:, None, None]
    next_third = atom_bit(third, 1)[:, None, None]
    allowed = (1.0 - last_first * head_second) * (1.0 - last_second * head_third)
    pairs = near_first * head_second + last_first * next_second + near_second * head_third + last_second * next_third
    angle = phase_third[:, None, None] + phase_second[None, :, None] + phase_first[None, None, :] + pair_angle * pairs
    return allowed, angle


def apply_third(real_part, imag_part, prop):
    def product(values, matrix):
        return jnp.einsum("ij,jba->iba", matrix, values, precision=lax.Precision.HIGHEST)
    return (product(real_part, prop[0]) - product(imag_part, prop[1]),
            product(real_part, prop[1]) + product(imag_part, prop[0]))


def apply_phases(real_part, imag_part, allowed, angle):
    cosine = jnp.cos(angle)
    sine = jnp.sin(angle)
    return (allowed * (real_part * cosine + imag_part * sine),
            allowed * (imag_part * cosine - real_part * sine))


def inner_rows(left, right):
    return lax.dot_general(left, right, (((0,), (0,)), ((), ())), precision=lax.Precision.HIGHEST,
                           preferred_element_type=jnp.float32)


def reference(amplitudes, prop_third, bitmasks_first, bitmasks_second, bitmasks_third, detune_steps):
    allowed, angle = boundary_terms(bitmasks_first, bitmasks_second, bitmasks_third, detune_steps)
    real_part, imag_part = apply_phases(amplitudes[0], amplitudes[1], allowed, angle)
    real_part, imag_part = apply_third(real_part, imag_part, prop_third)
    width = real_part.shape[2]
    flat_real = real_part.reshape(-1, width)
    flat_imag = imag_part.reshape(-1, width)
    density_real = inner_rows(flat_real, flat_real) + inner_rows(flat_imag, flat_imag)
    density_imag = inner_rows(flat_imag, flat_real) - inner_rows(flat_real, flat_imag)
    return jnp.stack([density_real, density_imag], axis=1)
```

```python
import functools
import jax
import jax.numpy as jnp
from jax import lax
from jax.experimental import pallas as pl
from jax.experimental.pallas import tpu as pltpu
from jax.sharding import PartitionSpec as P

angle_step = 0.2
pair_angle = 0.7
atom_count = 14
MESH = pl.DeviceIdType.MESH


def atom_bit(bitmasks, which):
    return (jnp.right_shift(bitmasks, which) & 1).astype(jnp.float32)


def occupation(bitmasks):
    total = jnp.zeros(bitmasks.shape, jnp.float32)
    for which in range(atom_count):
        total = total + atom_bit(bitmasks, which)
    return total


def factor_tables(first, second, third, detune_steps):
    scaled = detune_steps.astype(jnp.float32) * angle_step
    phase_first = scaled[0] * occupation(first)
    phase_second = scaled[1] * occupation(second)
    phase_third = scaled[2] * occupation(third)
    head, following = atom_bit(second, 0)[:, None], atom_bit(second, 1)[:, None]
    near, last = atom_bit(second, 12)[None, :], atom_bit(second, 13)[None, :]
    angle_ba = (
        phase_second[:, None]
        + phase_first[None, :]
        + pair_angle * (atom_bit(first, 12)[None, :] * head + atom_bit(first, 13)[None, :] * following)
    )
    allowed_ba = 1.0 - atom_bit(first, 13)[None, :] * head
    angle_cb = phase_third[:, None] + pair_angle * (
        near * atom_bit(third, 0)[:, None] + last * atom_bit(third, 1)[:, None]
    )
    allowed_cb = 1.0 - last * atom_bit(third, 0)[:, None]
    return lax.optimization_barrier(
        (
            allowed_ba * jnp.cos(angle_ba),
            allowed_ba * jnp.sin(angle_ba),
            allowed_cb * jnp.cos(angle_cb),
            allowed_cb * jnp.sin(angle_cb),
        )
    )


def apply_phases(amplitudes, tables):
    cos_ba, sin_ba, cos_cb, sin_cb = tables
    cos_cb, sin_cb = cos_cb[:, :, None], sin_cb[:, :, None]
    cosine = cos_ba[None] * cos_cb - sin_ba[None] * sin_cb
    sine = sin_ba[None] * cos_cb + cos_ba[None] * sin_cb
    return jnp.stack(
        [
            amplitudes[0] * cosine + amplitudes[1] * sine,
            amplitudes[1] * cosine - amplitudes[0] * sine,
        ]
    )


def split(values):
    high = values.astype(jnp.bfloat16)
    return high, (values - high.astype(jnp.float32)).astype(jnp.bfloat16)


def dot3(left, right, dims):
    def one(a, b):
        return lax.dot_general(a, b, (dims, ((), ())), preferred_element_type=jnp.float32)

    return one(left[0], right[0]) + (one(left[0], right[1]) + one(left[1], right[0]))


def density_kernel(
    n, x_ref, ah_ref, al_ref, out_ref,
    recv, xh, xl, vh, vl, total, kept, landing,
    send_sem, recv_sem, half_send, half_recv,
):
    steps = half_send.shape[0]
    me = lax.axis_index("cfg")
    each_b, rows_c = x_ref.shape[1], x_ref.shape[3]
    width = x_ref.shape[4]
    height = recv.shape[2]
    rows = out_ref.shape[1]

    barrier = pltpu.get_barrier_semaphore()

    def greet(s, carry):
        pl.semaphore_signal(
            barrier, inc=1, device_id={"cfg": lax.rem(me + s, n)}, device_id_type=MESH
        )
        return carry

    lax.fori_loop(1, n, greet, 0)
    pl.semaphore_wait(barrier, n - 1)

    def place(b):
        return recv.at[b, :, pl.ds(pl.multiple_of(me * rows_c, rows_c), rows_c), :]

    def send(b, s):
        peer = lax.rem(me + s, n)
        pltpu.make_async_remote_copy(
            src_ref=x_ref.at[peer, b],
            dst_ref=place(b),
            send_sem=send_sem.at[b],
            recv_sem=recv_sem.at[b],
            device_id={"cfg": peer},
            device_id_type=MESH,
        ).start()

    def send_all(b, carry):
        pltpu.make_async_copy(x_ref.at[me, b], place(b), recv_sem.at[b]).start()

        def pair(s, inner):
            send(b, n // 2 + s)
            send(b, n // 2 - s)
            return inner

        send(b, n // 2)
        lax.fori_loop(1, n // 2, pair, 0)
        return carry

    lax.fori_loop(0, each_b, send_all, 0)
    total[...] = jnp.zeros_like(total)

    tile = 256
    pairs_per_tile = tile // (2 * rows)

    def work(b, carry):
        pltpu.make_async_copy(recv.at[b], recv.at[b], recv_sem.at[b]).wait()

        for part in range(2):
            def split_rows(t, inner):
                at = pl.ds(pl.multiple_of(t * 64, 64), 64)
                to = pl.ds(pl.multiple_of(part * height + t * 64, 64), 64)
                high, low = split(recv[b, part, at, :])
                xh[to, :] = high
                xl[to, :] = low
                return inner

            lax.fori_loop(0, height // 64, split_rows, 0)

        def evolve(t, inner):
            at = pl.ds(pl.multiple_of(t * tile, tile), tile)
            value = dot3(
                (ah_ref[at, :], al_ref[at, :]), (xh[...], xl[...]), ((1,), (0,))
            )
            high, low = split(value)
            vh[at, :] = high
            vl[at, :] = low
            return inner

        lax.fori_loop(0, 2 * height // tile, evolve, 0)

        for t in range(width // tile):
            at = slice(t * tile, (t + 1) * tile)
            real = (vh[:height, :], vl[:height, :])
            imag = (vh[height:, :], vl[height:, :])
            real_t = (vh[:height, at], vl[:height, at])
            imag_t = (vh[height:, at], vl[height:, at])
            dims = ((0,), (0,))
            term_real = dot3(real_t, real, dims) + dot3(imag_t, imag, dims)
            to = slice(t * pairs_per_tile, (t + 1) * pairs_per_tile)
            shape = (pairs_per_tile, 2, rows, width)
            total[0, to] += term_real.reshape(shape)
            term_imag = dot3(imag_t, real, dims) - dot3(real_t, imag, dims)
            total[1, to] += term_imag.reshape(shape)
        return carry

    lax.fori_loop(0, each_b, work, 0)

    def halve(step, src, half):
        other = me + (1 - 2 * lax.rem(me // (2 ** step), 2)) * (2 ** step)
        copy = pltpu.make_async_remote_copy(
            src_ref=src,
            dst_ref=landing.at[:, pl.ds(n - 2 * half, half)],
            send_sem=half_send.at[step],
            recv_sem=half_recv.at[step],
            device_id={"cfg": other},
            device_id_type=MESH,
        )
        copy.start()
        return copy

    half = n // 2
    bit = lax.rem(me, 2)
    copy = halve(0, total.at[:, :, 1 - bit], half)
    copy.wait()

    def add_first(i, carry):
        where = 0
        rest = i
        for _ in range(steps - 1):
            where = where * 2 + lax.rem(rest, 2)
            rest = rest // 2
        kept[:, where] = total[:, i, bit] + landing[:, i]
        return carry

    lax.fori_loop(0, half, add_first, 0)
    offset = 0
    for step in range(1, steps):
        half = half // 2
        bit = lax.rem(me // (2 ** step), 2)
        copy = halve(step, kept.at[:, pl.ds(offset + (1 - bit) * half, half)], half)
        offset = offset + bit * half
        copy.wait()

        def add_next(i, carry, offset=offset, half=half):
            kept[:, offset + i] += landing[:, n - 2 * half + i]
            return carry

        lax.fori_loop(0, half, add_next, 0)
    out_ref[...] = kept[:, offset]

    for b in range(each_b):
        pltpu.make_async_copy(
            x_ref.at[pl.ds(0, n - 1), b], x_ref.at[pl.ds(0, n - 1), b], send_sem.at[b]
        ).wait()


def fused_density(phased, prop, n):
    _, rows_c, total_b, width = phased.shape
    height = prop.shape[1]
    each_b = total_b // n
    rows = width // n
    steps = n.bit_length() - 1
    outgoing = jnp.transpose(phased, (2, 0, 1, 3)).reshape(n, each_b, 2, rows_c, width)
    joined = jnp.concatenate(
        [
            jnp.concatenate([prop[0], -prop[1]], axis=1),
            jnp.concatenate([prop[1], prop[0]], axis=1),
        ],
        axis=0,
    )
    high = lax.reduce_precision(joined, 8, 7)
    low = (joined - high).astype(jnp.bfloat16)
    high = high.astype(jnp.bfloat16)
    vmem = pl.BlockSpec(memory_space=pltpu.VMEM)
    result = pl.pallas_call(
        functools.partial(density_kernel, n),
        out_shape=jax.ShapeDtypeStruct((2, rows, width), jnp.float32),
        in_specs=[pl.BlockSpec(memory_space=pl.ANY), vmem, vmem],
        out_specs=vmem,
        scratch_shapes=[
            pltpu.VMEM((each_b, 2, height, width), jnp.float32),
            pltpu.VMEM((2 * height, width), jnp.bfloat16),
            pltpu.VMEM((2 * height, width), jnp.bfloat16),
            pltpu.VMEM((2 * height, width), jnp.bfloat16),
            pltpu.VMEM((2 * height, width), jnp.bfloat16),
            pltpu.VMEM((2, n // 2, 2, rows, width), jnp.float32),
            pltpu.VMEM((2, n // 2, rows, width), jnp.float32),
            pltpu.VMEM((2, n - 1, rows, width), jnp.float32),
            pltpu.SemaphoreType.DMA((each_b,)),
            pltpu.SemaphoreType.DMA((each_b,)),
            pltpu.SemaphoreType.DMA((steps,)),
            pltpu.SemaphoreType.DMA((steps,)),
        ],
        compiler_params=pltpu.CompilerParams(
            collective_id=0, has_side_effects=True, vmem_limit_bytes=50 * 2**20
        ),
    )(outgoing, high, low)
    return jnp.transpose(result, (1, 0, 2))


def plain_density(phased, prop):
    def product(values, matrix):
        return jnp.einsum("ij,jba->iba", matrix, values, precision=lax.Precision.HIGHEST)

    def inner_rows(left, right):
        return lax.dot_general(
            left,
            right,
            (((0,), (0,)), ((), ())),
            precision=lax.Precision.HIGHEST,
            preferred_element_type=jnp.float32,
        )

    block = lax.all_to_all(phased, "cfg", split_axis=2, concat_axis=1, tiled=True)
    width = block.shape[3]
    real = (product(block[0], prop[0]) - product(block[1], prop[1])).reshape(-1, width)
    imag = (product(block[0], prop[1]) + product(block[1], prop[0])).reshape(-1, width)
    stacked = jnp.concatenate([real, imag], axis=0)
    crossed = inner_rows(imag, real)
    term = jnp.stack([inner_rows(stacked, stacked), crossed - crossed.T], axis=1)
    return lax.psum_scatter(term, "cfg", scatter_dimension=0, tiled=True)


def shards(n, amplitudes, prop_third, first, second, third, detune_steps):
    phased = apply_phases(amplitudes, factor_tables(first, second, third, detune_steps))
    _, rows_c, total_b, width = phased.shape
    height = prop_third.shape[1]
    fits = (
        n > 1
        and n & (n - 1) == 0
        and total_b % n == 0
        and rows_c % 8 == 0
        and width % (8 * n) == 0
        and width % 256 == 0
        and height % 256 == 0
        and 256 % (2 * (width // n)) == 0
        and 4 * total_b // n * height * width * 2 <= 2**24
    )
    if fits:
        return fused_density(phased, prop_third, n)
    return plain_density(phased, prop_third)


def solution(mesh):
    placed = (P("runs", "cfg", None, None), P(), P(), P(), P("cfg"), P("runs"))
    return jax.shard_map(
        functools.partial(shards, mesh.shape["cfg"]),
        mesh=mesh,
        in_specs=placed,
        out_specs=P(("runs", "cfg"), None, None),
        check_vma=False,
    )
```

```python
import functools
import jax
import jax.numpy as jnp
from jax import lax
from jax.experimental import pallas as pl
from jax.experimental.pallas import tpu as pltpu
from jax.sharding import PartitionSpec as P

angle_step = 0.2
pair_angle = 0.7
atom_count = 14
MESH = pl.DeviceIdType.MESH


def atom_bit(bitmasks, which):
    return (jnp.right_shift(bitmasks, which) & 1).astype(jnp.float32)


def occupation(bitmasks):
    total = jnp.zeros(bitmasks.shape, jnp.float32)
    for which in range(atom_count):
        total = total + atom_bit(bitmasks, which)
    return total


def factor_tables(first, second, third, detune_steps):
    scaled = detune_steps.astype(jnp.float32) * angle_step
    phase_first = scaled[0] * occupation(first)
    phase_second = scaled[1] * occupation(second)
    phase_third = scaled[2] * occupation(third)
    head, following = atom_bit(second, 0)[:, None], atom_bit(second, 1)[:, None]
    near, last = atom_bit(second, 12)[None, :], atom_bit(second, 13)[None, :]
    angle_ba = (
        phase_second[:, None]
        + phase_first[None, :]
        + pair_angle * (atom_bit(first, 12)[None, :] * head + atom_bit(first, 13)[None, :] * following)
    )
    allowed_ba = 1.0 - atom_bit(first, 13)[None, :] * head
    angle_cb = phase_third[:, None] + pair_angle * (
        near * atom_bit(third, 0)[:, None] + last * atom_bit(third, 1)[:, None]
    )
    allowed_cb = 1.0 - last * atom_bit(third, 0)[:, None]
    return lax.optimization_barrier(
        (
            allowed_ba * jnp.cos(angle_ba),
            allowed_ba * jnp.sin(angle_ba),
            allowed_cb * jnp.cos(angle_cb),
            allowed_cb * jnp.sin(angle_cb),
        )
    )


def apply_phases(amplitudes, tables):
    cos_ba, sin_ba, cos_cb, sin_cb = tables
    cos_cb, sin_cb = cos_cb[:, :, None], sin_cb[:, :, None]
    cosine = cos_ba[None] * cos_cb - sin_ba[None] * sin_cb
    sine = sin_ba[None] * cos_cb + cos_ba[None] * sin_cb
    return jnp.stack(
        [
            amplitudes[0] * cosine + amplitudes[1] * sine,
            amplitudes[1] * cosine - amplitudes[0] * sine,
        ]
    )


def split(values):
    high = values.astype(jnp.bfloat16)
    return high, (values - high.astype(jnp.float32)).astype(jnp.bfloat16)


def dot3(left, right, dims):
    def one(a, b):
        return lax.dot_general(a, b, (dims, ((), ())), preferred_element_type=jnp.float32)

    return one(left[0], right[0]) + (one(left[0], right[1]) + one(left[1], right[0]))


def column(row):
    size = row.shape[1]
    at = lax.broadcasted_iota(jnp.int32, (size, size), 0)
    across = lax.broadcasted_iota(jnp.int32, (size, size), 1)
    picked = jnp.where(at == across, row.astype(jnp.float32), 0.0)
    return jnp.sum(picked, axis=1, keepdims=True)


def density_kernel(
    n, amp_hbm, prop_hbm, first_ref, second_ref, third_ref, detune_ref, out_ref,
    amp, prop, second_col, cos_ba, sin_ba, cos_cb, sin_cb, outgoing, ah_ref, al_ref,
    recv, xh, xl, vh, vl, total, kept, landing,
    load_sem, send_sem, recv_sem, half_send, half_recv,
):
    steps = half_send.shape[0]
    me = lax.axis_index("cfg")
    total_b, _, rows_c, width = outgoing.shape
    each_b = total_b // n
    height = recv.shape[2]
    rows = out_ref.shape[1]

    load_amp = pltpu.make_async_copy(amp_hbm, amp, load_sem.at[0])
    load_prop = pltpu.make_async_copy(prop_hbm, prop, load_sem.at[1])
    load_amp.start()
    load_prop.start()

    barrier = pltpu.get_barrier_semaphore()

    def greet(s, carry):
        pl.semaphore_signal(
            barrier, inc=1, device_id={"cfg": lax.rem(me + s, n)}, device_id_type=MESH
        )
        return carry

    lax.fori_loop(1, n, greet, 0)

    def scaled(which):
        return detune_ref[which].astype(jnp.float32) * angle_step

    first, second = first_ref[...], second_ref[...]
    third = column(third_ref[...]).astype(jnp.int32)
    near, last = atom_bit(second, 12), atom_bit(second, 13)
    angle_cb = scaled(2) * occupation(third) + pair_angle * (
        near * atom_bit(third, 0) + last * atom_bit(third, 1)
    )
    allowed_cb = 1.0 - last * atom_bit(third, 0)
    cos_cb[...] = allowed_cb * jnp.cos(angle_cb)
    sin_cb[...] = allowed_cb * jnp.sin(angle_cb)
    second_col[...] = jnp.broadcast_to(column(second), second_col.shape)
    phase_first = scaled(0) * occupation(first)
    near_first, last_first = atom_bit(first, 12), atom_bit(first, 13)
    step_second = scaled(1)

    def table_rows(i, carry):
        at = pl.ds(pl.multiple_of(i * 8, 8), 8)
        mask = second_col[at, :][:, :1].astype(jnp.int32)
        head, following = atom_bit(mask, 0), atom_bit(mask, 1)
        angle = (
            step_second * occupation(mask)
            + phase_first
            + pair_angle * (near_first * head + last_first * following)
        )
        allowed = 1.0 - last_first * head
        cosine, sine = allowed * jnp.cos(angle), allowed * jnp.sin(angle)
        for k in range(width // 128):
            cos_ba[k, at, :] = cosine[:, k * 128 : (k + 1) * 128]
            sin_ba[k, at, :] = sine[:, k * 128 : (k + 1) * 128]
        return carry

    lax.fori_loop(0, total_b // 8, table_rows, 0)

    lane = lax.broadcasted_iota(jnp.int32, (rows_c, total_b), 1)
    columns = width // 128
    stride = total_b * columns

    def produce(b):
        here = lane == b
        cos_c = jnp.sum(jnp.where(here, cos_cb[...], 0.0), axis=1, keepdims=True)
        sin_c = jnp.sum(jnp.where(here, sin_cb[...], 0.0), axis=1, keepdims=True)
        for k in range(columns):
            lanes = slice(k * 128, (k + 1) * 128)
            start = ((b // 8) * columns + k) * 8 + lax.rem(b, 8)
            real = amp[0, pl.ds(start, rows_c, stride=stride), :]
            imag = amp[1, pl.ds(start, rows_c, stride=stride), :]
            cos_b = cos_ba[k, pl.ds(b, 1), :]
            sin_b = sin_ba[k, pl.ds(b, 1), :]
            cosine = cos_b * cos_c - sin_b * sin_c
            sine = sin_b * cos_c + cos_b * sin_c
            outgoing[b, 0, :, lanes] = real * cosine + imag * sine
            outgoing[b, 1, :, lanes] = imag * cosine - real * sine

    def place(j):
        return recv.at[j, :, pl.ds(pl.multiple_of(me * rows_c, rows_c), rows_c), :]

    def partner(i):
        return lax.rem(me + n // 2 + ((i + 1) // 2) * (1 - 2 * lax.rem(i, 2)), n)

    def send(i, j):
        peer = partner(i)
        pltpu.make_async_remote_copy(
            src_ref=outgoing.at[peer * each_b + j],
            dst_ref=place(j),
            send_sem=send_sem.at[j],
            recv_sem=recv_sem.at[j],
            device_id={"cfg": peer},
            device_id_type=MESH,
        ).start()

    load_amp.wait()
    pl.semaphore_wait(barrier, n - 1)

    def send_all(j, carry):
        produce(me * each_b + j)
        produce(partner(0) * each_b + j)

        def next_pair(i, inner):
            produce(partner(i) * each_b + j)
            send(i - 1, j)
            return inner

        lax.fori_loop(1, n - 1, next_pair, 0)
        pltpu.make_async_copy(
            outgoing.at[me * each_b + j], place(j), recv_sem.at[j]
        ).start()
        send(n - 2, j)
        return carry

    lax.fori_loop(0, each_b, send_all, 0)
    load_prop.wait()

    def split_prop(i, carry):
        at = pl.ds(pl.multiple_of(i * 64, 64), 64)
        below = pl.ds(pl.multiple_of(height + i * 64, 64), 64)
        high, low = split(prop[0, at, :])
        ah_ref[at, :height] = high
        al_ref[at, :height] = low
        ah_ref[below, height:] = high
        al_ref[below, height:] = low
        high, low = split(prop[1, at, :])
        ah_ref[at, height:] = -high
        al_ref[at, height:] = -low
        ah_ref[below, :height] = high
        al_ref[below, :height] = low
        return carry

    lax.fori_loop(0, height // 64, split_prop, 0)
    total[...] = jnp.zeros_like(total)

    tile = 256
    pairs_per_tile = tile // (2 * rows)

    def work(b, carry):
        pltpu.make_async_copy(recv.at[b], recv.at[b], recv_sem.at[b]).wait()

        for part in range(2):
            def split_rows(t, inner):
                at = pl.ds(pl.multiple_of(t * 64, 64), 64)
                to = pl.ds(pl.multiple_of(part * height + t * 64, 64), 64)
                high, low = split(recv[b, part, at, :])
                xh[to, :] = high
                xl[to, :] = low
                return inner

            lax.fori_loop(0, height // 64, split_rows, 0)

        def evolve(t, inner):
            at = pl.ds(pl.multiple_of(t * tile, tile), tile)
            value = dot3(
                (ah_ref[at, :], al_ref[at, :]), (xh[...], xl[...]), ((1,), (0,))
            )
            high, low = split(value)
            vh[at, :] = high
            vl[at, :] = low
            return inner

        lax.fori_loop(0, 2 * height // tile, evolve, 0)

        for t in range(width // tile):
            at = slice(t * tile, (t + 1) * tile)
            real = (vh[:height, :], vl[:height, :])
            imag = (vh[height:, :], vl[height:, :])
            real_t = (vh[:height, at], vl[:height, at])
            imag_t = (vh[height:, at], vl[height:, at])
            dims = ((0,), (0,))
            term_real = dot3(real_t, real, dims) + dot3(imag_t, imag, dims)
            to = slice(t * pairs_per_tile, (t + 1) * pairs_per_tile)
            shape = (pairs_per_tile, 2, rows, width)
            total[0, to] += term_real.reshape(shape)
            term_imag = dot3(imag_t, real, dims) - dot3(real_t, imag, dims)
            total[1, to] += term_imag.reshape(shape)
        return carry

    lax.fori_loop(0, each_b, work, 0)

    def halve(step, src, half):
        other = me + (1 - 2 * lax.rem(me // (2 ** step), 2)) * (2 ** step)
        copy = pltpu.make_async_remote_copy(
            src_ref=src,
            dst_ref=landing.at[:, pl.ds(n - 2 * half, half)],
            send_sem=half_send.at[step],
            recv_sem=half_recv.at[step],
            device_id={"cfg": other},
            device_id_type=MESH,
        )
        copy.start()
        return copy

    half = n // 2
    bit = lax.rem(me, 2)
    copy = halve(0, total.at[:, :, 1 - bit], half)
    copy.wait()

    def add_first(i, carry):
        where = 0
        rest = i
        for _ in range(steps - 1):
            where = where * 2 + lax.rem(rest, 2)
            rest = rest // 2
        kept[:, where] = total[:, i, bit] + landing[:, i]
        return carry

    lax.fori_loop(0, half, add_first, 0)
    offset = 0
    for step in range(1, steps):
        half = half // 2
        bit = lax.rem(me // (2 ** step), 2)
        copy = halve(step, kept.at[:, pl.ds(offset + (1 - bit) * half, half)], half)
        offset = offset + bit * half
        copy.wait()

        def add_next(i, carry, offset=offset, half=half):
            kept[:, offset + i] += landing[:, n - 2 * half + i]
            return carry

        lax.fori_loop(0, half, add_next, 0)
    out_ref[...] = kept[:, offset]

    for j in range(each_b):
        pltpu.make_async_copy(
            outgoing.at[pl.ds(0, n - 1)], outgoing.at[pl.ds(0, n - 1)], send_sem.at[j]
        ).wait()


def fused_density(amplitudes, prop, first, second, third, detune_steps, n):
    _, rows_c, total_b, width = amplitudes.shape
    height = prop.shape[1]
    each_b = total_b // n
    rows = width // n
    steps = n.bit_length() - 1
    tiled = amplitudes.reshape(2, rows_c, total_b // 8, 8, width // 128, 128)
    tiled = jnp.transpose(tiled, (0, 1, 2, 4, 3, 5)).reshape(2, -1, 128)
    vmem = pl.BlockSpec(memory_space=pltpu.VMEM)
    anywhere = pl.BlockSpec(memory_space=pl.ANY)
    result = pl.pallas_call(
        functools.partial(density_kernel, n),
        out_shape=jax.ShapeDtypeStruct((2, rows, width), jnp.float32),
        in_specs=[anywhere, anywhere, vmem, vmem, vmem, pl.BlockSpec(memory_space=pltpu.SMEM)],
        out_specs=vmem,
        scratch_shapes=[
            pltpu.VMEM(tiled.shape, jnp.float32),
            pltpu.VMEM(prop.shape, jnp.float32),
            pltpu.VMEM((total_b, 128), jnp.float32),
            pltpu.VMEM((width // 128, total_b, 128), jnp.float32),
            pltpu.VMEM((width // 128, total_b, 128), jnp.float32),
            pltpu.VMEM((rows_c, total_b), jnp.float32),
            pltpu.VMEM((rows_c, total_b), jnp.float32),
            pltpu.VMEM((total_b, 2, rows_c, width), jnp.float32),
            pltpu.VMEM((2 * height, 2 * height), jnp.bfloat16),
            pltpu.VMEM((2 * height, 2 * height), jnp.bfloat16),
            pltpu.VMEM((each_b, 2, height, width), jnp.float32),
            pltpu.VMEM((2 * height, width), jnp.bfloat16),
            pltpu.VMEM((2 * height, width), jnp.bfloat16),
            pltpu.VMEM((2 * height, width), jnp.bfloat16),
            pltpu.VMEM((2 * height, width), jnp.bfloat16),
            pltpu.VMEM((2, n // 2, 2, rows, width), jnp.float32),
            pltpu.VMEM((2, n // 2, rows, width), jnp.float32),
            pltpu.VMEM((2, n - 1, rows, width), jnp.float32),
            pltpu.SemaphoreType.DMA((2,)),
            pltpu.SemaphoreType.DMA((each_b,)),
            pltpu.SemaphoreType.DMA((each_b,)),
            pltpu.SemaphoreType.DMA((steps,)),
            pltpu.SemaphoreType.DMA((steps,)),
        ],
        compiler_params=pltpu.CompilerParams(
            collective_id=0, has_side_effects=True, vmem_limit_bytes=56 * 2**20
        ),
    )(
        tiled, prop, first.reshape(1, -1), second.reshape(1, -1), third.reshape(1, -1), detune_steps
    )
    return jnp.transpose(result, (1, 0, 2))


def plain_density(phased, prop):
    def product(values, matrix):
        return jnp.einsum("ij,jba->iba", matrix, values, precision=lax.Precision.HIGHEST)

    def inner_rows(left, right):
        return lax.dot_general(
            left,
            right,
            (((0,), (0,)), ((), ())),
            precision=lax.Precision.HIGHEST,
            preferred_element_type=jnp.float32,
        )

    block = lax.all_to_all(phased, "cfg", split_axis=2, concat_axis=1, tiled=True)
    width = block.shape[3]
    real = (product(block[0], prop[0]) - product(block[1], prop[1])).reshape(-1, width)
    imag = (product(block[0], prop[1]) + product(block[1], prop[0])).reshape(-1, width)
    stacked = jnp.concatenate([real, imag], axis=0)
    crossed = inner_rows(imag, real)
    term = jnp.stack([inner_rows(stacked, stacked), crossed - crossed.T], axis=1)
    return lax.psum_scatter(term, "cfg", scatter_dimension=0, tiled=True)


def shards(n, amplitudes, prop_third, first, second, third, detune_steps):
    _, rows_c, total_b, width = amplitudes.shape
    height = prop_third.shape[1]
    fits = (
        n > 1
        and n & (n - 1) == 0
        and total_b % n == 0
        and total_b % 128 == 0
        and rows_c % 8 == 0
        and width % (8 * n) == 0
        and width % 256 == 0
        and height % 256 == 0
        and 256 % (2 * (width // n)) == 0
        and 12 * rows_c * total_b * width <= 2**24
    )
    if fits:
        return fused_density(
            amplitudes, prop_third, first, second, third, detune_steps, n
        )
    phased = apply_phases(amplitudes, factor_tables(first, second, third, detune_steps))
    return plain_density(phased, prop_third)


def solution(mesh):
    placed = (P("runs", "cfg", None, None), P(), P(), P(), P("cfg"), P("runs"))
    return jax.shard_map(
        functools.partial(shards, mesh.shape["cfg"]),
        mesh=mesh,
        in_specs=placed,
        out_specs=P(("runs", "cfg"), None, None),
        check_vma=False,
    )
```

```python
import functools
import jax
import jax.numpy as jnp
from jax import lax
from jax.experimental import pallas as pl
from jax.experimental.pallas import tpu as pltpu
from jax.sharding import PartitionSpec as P

angle_step = 0.2
pair_angle = 0.7
atom_count = 14
MESH = pl.DeviceIdType.MESH


def atom_bit(bitmasks, which):
    return (jnp.right_shift(bitmasks, which) & 1).astype(jnp.float32)


def occupation(bitmasks):
    total = jnp.zeros(bitmasks.shape, jnp.float32)
    for which in range(atom_count):
        total = total + atom_bit(bitmasks, which)
    return total


def factor_tables(first, second, third, detune_steps):
    scaled = detune_steps.astype(jnp.float32) * angle_step
    phase_first = scaled[0] * occupation(first)
    phase_second = scaled[1] * occupation(second)
    phase_third = scaled[2] * occupation(third)
    head, following = atom_bit(second, 0)[:, None], atom_bit(second, 1)[:, None]
    near, last = atom_bit(second, 12)[None, :], atom_bit(second, 13)[None, :]
    angle_ba = (
        phase_second[:, None]
        + phase_first[None, :]
        + pair_angle * (atom_bit(first, 12)[None, :] * head + atom_bit(first, 13)[None, :] * following)
    )
    allowed_ba = 1.0 - atom_bit(first, 13)[None, :] * head
    angle_cb = phase_third[:, None] + pair_angle * (
        near * atom_bit(third, 0)[:, None] + last * atom_bit(third, 1)[:, None]
    )
    allowed_cb = 1.0 - last * atom_bit(third, 0)[:, None]
    return lax.optimization_barrier(
        (
            allowed_ba * jnp.cos(angle_ba),
            allowed_ba * jnp.sin(angle_ba),
            allowed_cb * jnp.cos(angle_cb),
            allowed_cb * jnp.sin(angle_cb),
        )
    )


def apply_phases(amplitudes, tables):
    cos_ba, sin_ba, cos_cb, sin_cb = tables
    cos_cb, sin_cb = cos_cb[:, :, None], sin_cb[:, :, None]
    cosine = cos_ba[None] * cos_cb - sin_ba[None] * sin_cb
    sine = sin_ba[None] * cos_cb + cos_ba[None] * sin_cb
    return jnp.stack(
        [
            amplitudes[0] * cosine + amplitudes[1] * sine,
            amplitudes[1] * cosine - amplitudes[0] * sine,
        ]
    )


def split(values):
    high = values.astype(jnp.bfloat16)
    return high, (values - high.astype(jnp.float32)).astype(jnp.bfloat16)


def dot3(left, right, dims):
    def one(a, b):
        return lax.dot_general(a, b, (dims, ((), ())), preferred_element_type=jnp.float32)

    return one(left[0], right[0]) + (one(left[0], right[1]) + one(left[1], right[0]))


def column(row):
    size = row.shape[1]
    at = lax.broadcasted_iota(jnp.int32, (size, size), 0)
    across = lax.broadcasted_iota(jnp.int32, (size, size), 1)
    picked = jnp.where(at == across, row.astype(jnp.float32), 0.0)
    return jnp.sum(picked, axis=1, keepdims=True)


def part_order(part, steps):
    order = list(range(steps))
    if steps > 4:
        turned = [(1, 2, 3), (2, 1, 3), (3, 1, 2), (3, 2, 1)][part % 4]
        order[1:4] = turned
    return order


def density_kernel(
    n, amp_hbm, prop_hbm, first_ref, second_ref, third_ref, detune_ref, out_ref,
    amp, prop, second_col, cos_ba, sin_ba, cos_cb, sin_cb, outgoing, ah_ref, al_ref,
    recv, xh, xl, vh, vl, total, kept, landing,
    load_sem, send_sem, recv_sem, half_send, half_recv,
):
    steps = half_send.shape[1]
    me = lax.axis_index("cfg")
    total_b, _, rows_c, width = outgoing.shape
    each_b = total_b // n
    height = recv.shape[2]
    rows = out_ref.shape[1]

    load_amp = pltpu.make_async_copy(amp_hbm, amp, load_sem.at[0])
    load_prop = pltpu.make_async_copy(prop_hbm, prop, load_sem.at[1])
    load_amp.start()
    load_prop.start()

    barrier = pltpu.get_barrier_semaphore()

    def greet(s, carry):
        pl.semaphore_signal(
            barrier, inc=1, device_id={"cfg": lax.rem(me + s, n)}, device_id_type=MESH
        )
        return carry

    lax.fori_loop(1, n, greet, 0)

    def scaled(which):
        return detune_ref[which].astype(jnp.float32) * angle_step

    first, second = first_ref[...], second_ref[...]
    third = column(third_ref[...]).astype(jnp.int32)
    near, last = atom_bit(second, 12), atom_bit(second, 13)
    angle_cb = scaled(2) * occupation(third) + pair_angle * (
        near * atom_bit(third, 0) + last * atom_bit(third, 1)
    )
    allowed_cb = 1.0 - last * atom_bit(third, 0)
    cos_cb[...] = allowed_cb * jnp.cos(angle_cb)
    sin_cb[...] = allowed_cb * jnp.sin(angle_cb)
    second_col[...] = jnp.broadcast_to(column(second), second_col.shape)
    phase_first = scaled(0) * occupation(first)
    near_first, last_first = atom_bit(first, 12), atom_bit(first, 13)
    step_second = scaled(1)

    def table_rows(i, carry):
        at = pl.ds(pl.multiple_of(i * 8, 8), 8)
        mask = second_col[at, :][:, :1].astype(jnp.int32)
        head, following = atom_bit(mask, 0), atom_bit(mask, 1)
        angle = (
            step_second * occupation(mask)
            + phase_first
            + pair_angle * (near_first * head + last_first * following)
        )
        allowed = 1.0 - last_first * head
        cosine, sine = allowed * jnp.cos(angle), allowed * jnp.sin(angle)
        for k in range(width // 128):
            cos_ba[k, at, :] = cosine[:, k * 128 : (k + 1) * 128]
            sin_ba[k, at, :] = sine[:, k * 128 : (k + 1) * 128]
        return carry

    lax.fori_loop(0, total_b // 8, table_rows, 0)

    lane = lax.broadcasted_iota(jnp.int32, (rows_c, total_b), 1)
    columns = width // 128
    stride = total_b * columns

    def produce(b):
        here = lane == b
        cos_c = jnp.sum(jnp.where(here, cos_cb[...], 0.0), axis=1, keepdims=True)
        sin_c = jnp.sum(jnp.where(here, sin_cb[...], 0.0), axis=1, keepdims=True)
        for k in range(columns):
            lanes = slice(k * 128, (k + 1) * 128)
            start = ((b // 8) * columns + k) * 8 + lax.rem(b, 8)
            real = amp[0, pl.ds(start, rows_c, stride=stride), :]
            imag = amp[1, pl.ds(start, rows_c, stride=stride), :]
            cos_b = cos_ba[k, pl.ds(b, 1), :]
            sin_b = sin_ba[k, pl.ds(b, 1), :]
            cosine = cos_b * cos_c - sin_b * sin_c
            sine = sin_b * cos_c + cos_b * sin_c
            outgoing[b, 0, :, lanes] = real * cosine + imag * sine
            outgoing[b, 1, :, lanes] = imag * cosine - real * sine

    def place(j):
        return recv.at[j, :, pl.ds(pl.multiple_of(me * rows_c, rows_c), rows_c), :]

    def partner(i):
        return lax.rem(me + n // 2 + ((i + 1) // 2) * (1 - 2 * lax.rem(i, 2)), n)

    def send(i, j):
        peer = partner(i)
        pltpu.make_async_remote_copy(
            src_ref=outgoing.at[peer * each_b + j],
            dst_ref=place(j),
            send_sem=send_sem.at[j],
            recv_sem=recv_sem.at[j],
            device_id={"cfg": peer},
            device_id_type=MESH,
        ).start()

    load_amp.wait()
    pl.semaphore_wait(barrier, n - 1)

    def send_all(j, carry):
        produce(me * each_b + j)
        produce(partner(0) * each_b + j)

        def next_pair(i, inner):
            produce(partner(i) * each_b + j)
            send(i - 1, j)
            return inner

        lax.fori_loop(1, n - 1, next_pair, 0)
        pltpu.make_async_copy(
            outgoing.at[me * each_b + j], place(j), recv_sem.at[j]
        ).start()
        send(n - 2, j)
        return carry

    lax.fori_loop(0, each_b, send_all, 0)
    load_prop.wait()

    def split_prop(i, carry):
        at = pl.ds(pl.multiple_of(i * 64, 64), 64)
        below = pl.ds(pl.multiple_of(height + i * 64, 64), 64)
        high, low = split(prop[0, at, :])
        ah_ref[at, :height] = high
        al_ref[at, :height] = low
        ah_ref[below, height:] = high
        al_ref[below, height:] = low
        high, low = split(prop[1, at, :])
        ah_ref[at, height:] = -high
        al_ref[at, height:] = -low
        ah_ref[below, :height] = high
        al_ref[below, :height] = low
        return carry

    lax.fori_loop(0, height // 64, split_prop, 0)
    total[...] = jnp.zeros_like(total)

    tile = 256
    pairs_per_tile = tile // (2 * rows)

    def work(b, carry):
        pltpu.make_async_copy(recv.at[b], recv.at[b], recv_sem.at[b]).wait()

        for part in range(2):
            def split_rows(t, inner):
                at = pl.ds(pl.multiple_of(t * 64, 64), 64)
                to = pl.ds(pl.multiple_of(part * height + t * 64, 64), 64)
                high, low = split(recv[b, part, at, :])
                xh[to, :] = high
                xl[to, :] = low
                return inner

            lax.fori_loop(0, height // 64, split_rows, 0)

        def evolve(t, inner):
            at = pl.ds(pl.multiple_of(t * tile, tile), tile)
            value = dot3(
                (ah_ref[at, :], al_ref[at, :]), (xh[...], xl[...]), ((1,), (0,))
            )
            high, low = split(value)
            vh[at, :] = high
            vl[at, :] = low
            return inner

        lax.fori_loop(0, 2 * height // tile, evolve, 0)

        for t in range(width // tile):
            at = slice(t * tile, (t + 1) * tile)
            real = (vh[:height, :], vl[:height, :])
            imag = (vh[height:, :], vl[height:, :])
            real_t = (vh[:height, at], vl[:height, at])
            imag_t = (vh[height:, at], vl[height:, at])
            dims = ((0,), (0,))
            term_real = dot3(real_t, real, dims) + dot3(imag_t, imag, dims)
            to = slice(t * pairs_per_tile, (t + 1) * pairs_per_tile)
            shape = (pairs_per_tile, 2, rows, width)
            total[0, to] += term_real.reshape(shape)
            term_imag = dot3(imag_t, real, dims) - dot3(real_t, imag, dims)
            total[1, to] += term_imag.reshape(shape)
        return carry

    lax.fori_loop(0, each_b, work, 0)

    parts = width // 128
    orders = [part_order(p, steps) for p in range(parts)]
    offsets = [0] * parts

    def bit_of(index, which):
        return lax.rem(index // (2 ** which), 2)

    def halve(p, t):
        half = n >> (t + 1)
        which = orders[p][t]
        bit = bit_of(me, which)
        lanes = pl.ds(p * 128, 128)
        if t == 0:
            src = total.at[:, :, 1 - bit, :, lanes]
        else:
            src = kept.at[:, pl.ds(offsets[p] + (1 - bit) * half, half), :, lanes]
            offsets[p] = offsets[p] + bit * half
        copy = pltpu.make_async_remote_copy(
            src_ref=src,
            dst_ref=landing.at[:, pl.ds(n - 2 * half, half), :, lanes],
            send_sem=half_send.at[p, t],
            recv_sem=half_recv.at[p, t],
            device_id={"cfg": me + (1 - 2 * bit) * (2 ** which)},
            device_id_type=MESH,
        )
        copy.start()
        return copy

    def add(p, t):
        half = n >> (t + 1)
        lanes = slice(p * 128, (p + 1) * 128)
        if t == 0:
            core = bit_of(me, 0)

            def add_first(i, carry):
                where = 0
                for which in orders[p][1:]:
                    where = where * 2 + bit_of(i, which - 1)
                kept[:, where, :, lanes] = total[:, i, core, :, lanes] + landing[:, i, :, lanes]
                return carry

            lax.fori_loop(0, half, add_first, 0)
        else:
            first = n - 2 * half
            at = pl.ds(offsets[p], half)
            kept[:, at, :, lanes] += landing[:, first : first + half, :, lanes]

    flying = [halve(p, 0) for p in range(parts)]
    for t in range(steps):
        for p in range(parts):
            flying[p].wait()
            add(p, t)
            if t + 1 < steps:
                flying[p] = halve(p, t + 1)
            else:
                lanes = slice(p * 128, (p + 1) * 128)
                out_ref[:, :, lanes] = kept[:, offsets[p], :, lanes]

    for j in range(each_b):
        pltpu.make_async_copy(
            outgoing.at[pl.ds(0, n - 1)], outgoing.at[pl.ds(0, n - 1)], send_sem.at[j]
        ).wait()


def fused_density(amplitudes, prop, first, second, third, detune_steps, n):
    _, rows_c, total_b, width = amplitudes.shape
    height = prop.shape[1]
    each_b = total_b // n
    rows = width // n
    steps = n.bit_length() - 1
    tiled = amplitudes.reshape(2, rows_c, total_b // 8, 8, width // 128, 128)
    tiled = jnp.transpose(tiled, (0, 1, 2, 4, 3, 5)).reshape(2, -1, 128)
    vmem = pl.BlockSpec(memory_space=pltpu.VMEM)
    anywhere = pl.BlockSpec(memory_space=pl.ANY)
    result = pl.pallas_call(
        functools.partial(density_kernel, n),
        out_shape=jax.ShapeDtypeStruct((2, rows, width), jnp.float32),
        in_specs=[anywhere, anywhere, vmem, vmem, vmem, pl.BlockSpec(memory_space=pltpu.SMEM)],
        out_specs=vmem,
        scratch_shapes=[
            pltpu.VMEM(tiled.shape, jnp.float32),
            pltpu.VMEM(prop.shape, jnp.float32),
            pltpu.VMEM((total_b, 128), jnp.float32),
            pltpu.VMEM((width // 128, total_b, 128), jnp.float32),
            pltpu.VMEM((width // 128, total_b, 128), jnp.float32),
            pltpu.VMEM((rows_c, total_b), jnp.float32),
            pltpu.VMEM((rows_c, total_b), jnp.float32),
            pltpu.VMEM((total_b, 2, rows_c, width), jnp.float32),
            pltpu.VMEM((2 * height, 2 * height), jnp.bfloat16),
            pltpu.VMEM((2 * height, 2 * height), jnp.bfloat16),
            pltpu.VMEM((each_b, 2, height, width), jnp.float32),
            pltpu.VMEM((2 * height, width), jnp.bfloat16),
            pltpu.VMEM((2 * height, width), jnp.bfloat16),
            pltpu.VMEM((2 * height, width), jnp.bfloat16),
            pltpu.VMEM((2 * height, width), jnp.bfloat16),
            pltpu.VMEM((2, n // 2, 2, rows, width), jnp.float32),
            pltpu.VMEM((2, n // 2, rows, width), jnp.float32),
            pltpu.VMEM((2, n - 1, rows, width), jnp.float32),
            pltpu.SemaphoreType.DMA((2,)),
            pltpu.SemaphoreType.DMA((each_b,)),
            pltpu.SemaphoreType.DMA((each_b,)),
            pltpu.SemaphoreType.DMA((width // 128, steps)),
            pltpu.SemaphoreType.DMA((width // 128, steps)),
        ],
        compiler_params=pltpu.CompilerParams(
            collective_id=0, has_side_effects=True, vmem_limit_bytes=56 * 2**20
        ),
    )(
        tiled, prop, first.reshape(1, -1), second.reshape(1, -1), third.reshape(1, -1), detune_steps
    )
    return jnp.transpose(result, (1, 0, 2))


def plain_density(phased, prop):
    def product(values, matrix):
        return jnp.einsum("ij,jba->iba", matrix, values, precision=lax.Precision.HIGHEST)

    def inner_rows(left, right):
        return lax.dot_general(
            left,
            right,
            (((0,), (0,)), ((), ())),
            precision=lax.Precision.HIGHEST,
            preferred_element_type=jnp.float32,
        )

    block = lax.all_to_all(phased, "cfg", split_axis=2, concat_axis=1, tiled=True)
    width = block.shape[3]
    real = (product(block[0], prop[0]) - product(block[1], prop[1])).reshape(-1, width)
    imag = (product(block[0], prop[1]) + product(block[1], prop[0])).reshape(-1, width)
    stacked = jnp.concatenate([real, imag], axis=0)
    crossed = inner_rows(imag, real)
    term = jnp.stack([inner_rows(stacked, stacked), crossed - crossed.T], axis=1)
    return lax.psum_scatter(term, "cfg", scatter_dimension=0, tiled=True)


def shards(n, amplitudes, prop_third, first, second, third, detune_steps):
    _, rows_c, total_b, width = amplitudes.shape
    height = prop_third.shape[1]
    fits = (
        n > 1
        and n & (n - 1) == 0
        and total_b % n == 0
        and total_b % 128 == 0
        and rows_c % 8 == 0
        and width % (8 * n) == 0
        and width % 256 == 0
        and height % 256 == 0
        and 256 % (2 * (width // n)) == 0
        and 12 * rows_c * total_b * width <= 2**24
    )
    if fits:
        return fused_density(
            amplitudes, prop_third, first, second, third, detune_steps, n
        )
    phased = apply_phases(amplitudes, factor_tables(first, second, third, detune_steps))
    return plain_density(phased, prop_third)


def solution(mesh):
    placed = (P("runs", "cfg", None, None), P(), P(), P(), P("cfg"), P("runs"))
    return jax.shard_map(
        functools.partial(shards, mesh.shape["cfg"]),
        mesh=mesh,
        in_specs=placed,
        out_specs=P(("runs", "cfg"), None, None),
        check_vma=False,
    )
```

```python
import functools
import jax
import jax.numpy as jnp
from jax import lax
from jax.experimental import pallas as pl
from jax.experimental.pallas import tpu as pltpu
from jax.sharding import PartitionSpec as P

angle_step = 0.2
pair_angle = 0.7
atom_count = 14
MESH = pl.DeviceIdType.MESH


def atom_bit(bitmasks, which):
    return (jnp.right_shift(bitmasks, which) & 1).astype(jnp.float32)


def occupation(bitmasks):
    total = jnp.zeros(bitmasks.shape, jnp.float32)
    for which in range(atom_count):
        total = total + atom_bit(bitmasks, which)
    return total


def factor_tables(first, second, third, detune_steps):
    scaled = detune_steps.astype(jnp.float32) * angle_step
    phase_first = scaled[0] * occupation(first)
    phase_second = scaled[1] * occupation(second)
    phase_third = scaled[2] * occupation(third)
    head, following = atom_bit(second, 0)[:, None], atom_bit(second, 1)[:, None]
    near, last = atom_bit(second, 12)[None, :], atom_bit(second, 13)[None, :]
    angle_ba = (
        phase_second[:, None]
        + phase_first[None, :]
        + pair_angle * (atom_bit(first, 12)[None, :] * head + atom_bit(first, 13)[None, :] * following)
    )
    allowed_ba = 1.0 - atom_bit(first, 13)[None, :] * head
    angle_cb = phase_third[:, None] + pair_angle * (
        near * atom_bit(third, 0)[:, None] + last * atom_bit(third, 1)[:, None]
    )
    allowed_cb = 1.0 - last * atom_bit(third, 0)[:, None]
    return lax.optimization_barrier(
        (
            allowed_ba * jnp.cos(angle_ba),
            allowed_ba * jnp.sin(angle_ba),
            allowed_cb * jnp.cos(angle_cb),
            allowed_cb * jnp.sin(angle_cb),
        )
    )


def apply_phases(amplitudes, tables):
    cos_ba, sin_ba, cos_cb, sin_cb = tables
    cos_cb, sin_cb = cos_cb[:, :, None], sin_cb[:, :, None]
    cosine = cos_ba[None] * cos_cb - sin_ba[None] * sin_cb
    sine = sin_ba[None] * cos_cb + cos_ba[None] * sin_cb
    return jnp.stack(
        [
            amplitudes[0] * cosine + amplitudes[1] * sine,
            amplitudes[1] * cosine - amplitudes[0] * sine,
        ]
    )


def split(values):
    high = values.astype(jnp.bfloat16)
    return high, (values - high.astype(jnp.float32)).astype(jnp.bfloat16)


def dot3(left, right, dims):
    def one(a, b):
        return lax.dot_general(a, b, (dims, ((), ())), preferred_element_type=jnp.float32)

    return one(left[0], right[0]) + (one(left[0], right[1]) + one(left[1], right[0]))


def column(row):
    size = row.shape[1]
    at = lax.broadcasted_iota(jnp.int32, (size, size), 0)
    across = lax.broadcasted_iota(jnp.int32, (size, size), 1)
    picked = jnp.where(at == across, row.astype(jnp.float32), 0.0)
    return jnp.sum(picked, axis=1, keepdims=True)


def part_order(part, steps):
    order = list(range(steps))
    if steps > 4:
        turned = [(1, 2, 3), (2, 1, 3), (3, 1, 2), (3, 2, 1)][part % 4]
        order[1:4] = turned
    return order


def density_kernel(
    n, amp_hbm, prop_hbm, first_ref, second_ref, third_ref, detune_ref, out_ref,
    amp, prop, second_col, cos_ba, sin_ba, cos_cb, sin_cb, outgoing, ah_ref, al_ref,
    recv, xh, xl, vh, vl, total, kept, landing,
    load_sem, send_sem, recv_sem, half_send, half_recv,
):
    steps = half_send.shape[1]
    me = lax.axis_index("cfg")
    total_b, _, rows_c, width = outgoing.shape
    each_b = total_b // n
    height = recv.shape[2]
    rows = out_ref.shape[1]

    load_amp = pltpu.make_async_copy(amp_hbm, amp, load_sem.at[0])
    load_prop = pltpu.make_async_copy(prop_hbm, prop, load_sem.at[1])
    load_amp.start()
    load_prop.start()

    barrier = pltpu.get_barrier_semaphore()

    def greet(s, carry):
        pl.semaphore_signal(
            barrier, inc=1, device_id={"cfg": lax.rem(me + s, n)}, device_id_type=MESH
        )
        return carry

    lax.fori_loop(1, n, greet, 0)

    def scaled(which):
        return detune_ref[which].astype(jnp.float32) * angle_step

    first, second = first_ref[...], second_ref[...]
    third = column(third_ref[...]).astype(jnp.int32)
    near, last = atom_bit(second, 12), atom_bit(second, 13)
    angle_cb = scaled(2) * occupation(third) + pair_angle * (
        near * atom_bit(third, 0) + last * atom_bit(third, 1)
    )
    allowed_cb = 1.0 - last * atom_bit(third, 0)
    cos_cb[...] = allowed_cb * jnp.cos(angle_cb)
    sin_cb[...] = allowed_cb * jnp.sin(angle_cb)
    second_col[...] = jnp.broadcast_to(column(second), second_col.shape)
    phase_first = scaled(0) * occupation(first)
    near_first, last_first = atom_bit(first, 12), atom_bit(first, 13)
    step_second = scaled(1)

    def table_rows(i, carry):
        at = pl.ds(pl.multiple_of(i * 8, 8), 8)
        mask = second_col[at, :][:, :1].astype(jnp.int32)
        head, following = atom_bit(mask, 0), atom_bit(mask, 1)
        angle = (
            step_second * occupation(mask)
            + phase_first
            + pair_angle * (near_first * head + last_first * following)
        )
        allowed = 1.0 - last_first * head
        cosine, sine = allowed * jnp.cos(angle), allowed * jnp.sin(angle)
        for k in range(width // 128):
            cos_ba[k, at, :] = cosine[:, k * 128 : (k + 1) * 128]
            sin_ba[k, at, :] = sine[:, k * 128 : (k + 1) * 128]
        return carry

    lax.fori_loop(0, total_b // 8, table_rows, 0)

    lane = lax.broadcasted_iota(jnp.int32, (rows_c, total_b), 1)
    columns = width // 128
    stride = total_b * columns

    def produce(b):
        here = lane == b
        cos_c = jnp.sum(jnp.where(here, cos_cb[...], 0.0), axis=1, keepdims=True)
        sin_c = jnp.sum(jnp.where(here, sin_cb[...], 0.0), axis=1, keepdims=True)
        for k in range(columns):
            lanes = slice(k * 128, (k + 1) * 128)
            start = ((b // 8) * columns + k) * 8 + lax.rem(b, 8)
            real = amp[0, pl.ds(start, rows_c, stride=stride), :]
            imag = amp[1, pl.ds(start, rows_c, stride=stride), :]
            cos_b = cos_ba[k, pl.ds(b, 1), :]
            sin_b = sin_ba[k, pl.ds(b, 1), :]
            cosine = cos_b * cos_c - sin_b * sin_c
            sine = sin_b * cos_c + cos_b * sin_c
            outgoing[b, 0, :, lanes] = real * cosine + imag * sine
            outgoing[b, 1, :, lanes] = imag * cosine - real * sine

    def place(j, lanes):
        return recv.at[j, :, pl.ds(pl.multiple_of(me * rows_c, rows_c), rows_c), lanes]

    def partner(i):
        return lax.rem(me + n // 2 + ((i + 1) // 2) * (1 - 2 * lax.rem(i, 2)), n)

    def send(i, j, lanes, sem):
        peer = partner(i)
        pltpu.make_async_remote_copy(
            src_ref=outgoing.at[peer * each_b + j, :, :, lanes],
            dst_ref=place(j, lanes),
            send_sem=send_sem.at[sem],
            recv_sem=recv_sem.at[sem],
            device_id={"cfg": peer},
            device_id_type=MESH,
        ).start()

    def keep(j, lanes, sem):
        pltpu.make_async_copy(
            outgoing.at[me * each_b + j, :, :, lanes], place(j, lanes), recv_sem.at[sem]
        ).start()

    everything = pl.ds(0, width)
    near_half, far_half = pl.ds(0, width // 2), pl.ds(width // 2, width // 2)

    load_amp.wait()
    pl.semaphore_wait(barrier, n - 1)

    def produce_all(j, lanes, sem):
        produce(me * each_b + j)
        produce(partner(0) * each_b + j)

        def next_pair(i, inner):
            produce(partner(i) * each_b + j)
            send(i - 1, j, lanes, sem)
            return inner

        lax.fori_loop(1, n - 1, next_pair, 0)
        keep(j, lanes, sem)
        send(n - 2, j, lanes, sem)

    def send_all(j, carry):
        produce_all(j, everything, j)
        return carry

    final = each_b - 1
    lax.fori_loop(0, final, send_all, 0)
    produce_all(final, near_half, final)

    def send_rest(i, carry):
        send(i, final, far_half, final + 1)
        return carry

    lax.fori_loop(0, n - 1, send_rest, 0)
    keep(final, far_half, final + 1)
    load_prop.wait()

    def split_prop(i, carry):
        at = pl.ds(pl.multiple_of(i * 64, 64), 64)
        below = pl.ds(pl.multiple_of(height + i * 64, 64), 64)
        high, low = split(prop[0, at, :])
        ah_ref[at, :height] = high
        al_ref[at, :height] = low
        ah_ref[below, height:] = high
        al_ref[below, height:] = low
        high, low = split(prop[1, at, :])
        ah_ref[at, height:] = -high
        al_ref[at, height:] = -low
        ah_ref[below, :height] = high
        al_ref[below, :height] = low
        return carry

    lax.fori_loop(0, height // 64, split_prop, 0)
    total[...] = jnp.zeros_like(total)

    def arrived(b, lanes, sem):
        pltpu.make_async_copy(
            recv.at[b, :, :, lanes], recv.at[b, :, :, lanes], recv_sem.at[sem]
        ).wait()

    tile = 256

    def propagate(b, lanes):
        for part in range(2):
            def split_rows(t, inner):
                at = pl.ds(pl.multiple_of(t * 64, 64), 64)
                to = pl.ds(pl.multiple_of(part * height + t * 64, 64), 64)
                high, low = split(recv[b, part, at, lanes])
                xh[to, lanes] = high
                xl[to, lanes] = low
                return inner

            lax.fori_loop(0, height // 64, split_rows, 0)

        def evolve(t, inner):
            at = pl.ds(pl.multiple_of(t * tile, tile), tile)
            value = dot3(
                (ah_ref[at, :], al_ref[at, :]), (xh[:, lanes], xl[:, lanes]), ((1,), (0,))
            )
            high, low = split(value)
            vh[at, lanes] = high
            vl[at, lanes] = low
            return inner

        lax.fori_loop(0, 2 * height // tile, evolve, 0)

    def accumulate(left, right):
        def pieces(lanes):
            return (
                (vh[:height, lanes], vl[:height, lanes]),
                (vh[height:, lanes], vl[height:, lanes]),
            )

        real, imag = pieces(right)
        dims = ((0,), (0,))
        for at in range(left.start, left.stop, tile):
            real_t, imag_t = pieces(slice(at, at + tile))
            to = slice(at // (2 * rows), (at + tile) // (2 * rows))
            shape = (tile // (2 * rows), 2, rows, right.stop - right.start)
            term_real = dot3(real_t, real, dims) + dot3(imag_t, imag, dims)
            total[0, to, :, :, right] += term_real.reshape(shape)
            term_imag = dot3(imag_t, real, dims) - dot3(real_t, imag, dims)
            total[1, to, :, :, right] += term_imag.reshape(shape)

    middle = width // 2
    full, low_half, high_half = slice(0, width), slice(0, middle), slice(middle, width)

    def work(b, carry):
        arrived(b, everything, b)
        propagate(b, full)
        accumulate(full, full)
        return carry

    lax.fori_loop(0, final, work, 0)
    arrived(final, near_half, final)
    propagate(final, low_half)
    accumulate(low_half, low_half)
    arrived(final, far_half, final + 1)
    propagate(final, high_half)

    parts = width // 128
    orders = [part_order(p, steps) for p in range(parts)]
    offsets = [0] * parts

    def bit_of(index, which):
        return lax.rem(index // (2 ** which), 2)

    def halve(p, t):
        half = n >> (t + 1)
        which = orders[p][t]
        bit = bit_of(me, which)
        lanes = pl.ds(p * 128, 128)
        if t == 0:
            src = total.at[:, :, 1 - bit, :, lanes]
        else:
            src = kept.at[:, pl.ds(offsets[p] + (1 - bit) * half, half), :, lanes]
            offsets[p] = offsets[p] + bit * half
        copy = pltpu.make_async_remote_copy(
            src_ref=src,
            dst_ref=landing.at[:, pl.ds(n - 2 * half, half), :, lanes],
            send_sem=half_send.at[p, t],
            recv_sem=half_recv.at[p, t],
            device_id={"cfg": me + (1 - 2 * bit) * (2 ** which)},
            device_id_type=MESH,
        )
        copy.start()
        return copy

    def add(p, t):
        half = n >> (t + 1)
        lanes = slice(p * 128, (p + 1) * 128)
        if t == 0:
            core = bit_of(me, 0)

            def add_first(i, carry):
                where = 0
                for which in orders[p][1:]:
                    where = where * 2 + bit_of(i, which - 1)
                kept[:, where, :, lanes] = total[:, i, core, :, lanes] + landing[:, i, :, lanes]
                return carry

            lax.fori_loop(0, half, add_first, 0)
        else:
            first = n - 2 * half
            at = pl.ds(offsets[p], half)
            kept[:, at, :, lanes] += landing[:, first : first + half, :, lanes]

    flying = {}
    accumulate(full, high_half)
    for p in range(parts // 2, parts):
        flying[p] = halve(p, 0)
    accumulate(high_half, low_half)
    for p in range(parts // 2):
        flying[p] = halve(p, 0)
    for t in range(steps):
        for p in list(flying):
            flying[p].wait()
            add(p, t)
            if t + 1 < steps:
                flying[p] = halve(p, t + 1)
            else:
                lanes = slice(p * 128, (p + 1) * 128)
                out_ref[:, :, lanes] = kept[:, offsets[p], :, lanes]

    for j, lanes in enumerate([everything] * final + [near_half, far_half]):
        sent = outgoing.at[pl.ds(0, n - 1), :, :, lanes]
        pltpu.make_async_copy(sent, sent, send_sem.at[j]).wait()


def fused_density(amplitudes, prop, first, second, third, detune_steps, n):
    _, rows_c, total_b, width = amplitudes.shape
    height = prop.shape[1]
    each_b = total_b // n
    rows = width // n
    steps = n.bit_length() - 1
    tiled = amplitudes.reshape(2, rows_c, total_b // 8, 8, width // 128, 128)
    tiled = jnp.transpose(tiled, (0, 1, 2, 4, 3, 5)).reshape(2, -1, 128)
    vmem = pl.BlockSpec(memory_space=pltpu.VMEM)
    anywhere = pl.BlockSpec(memory_space=pl.ANY)
    result = pl.pallas_call(
        functools.partial(density_kernel, n),
        out_shape=jax.ShapeDtypeStruct((2, rows, width), jnp.float32),
        in_specs=[anywhere, anywhere, vmem, vmem, vmem, pl.BlockSpec(memory_space=pltpu.SMEM)],
        out_specs=vmem,
        scratch_shapes=[
            pltpu.VMEM(tiled.shape, jnp.float32),
            pltpu.VMEM(prop.shape, jnp.float32),
            pltpu.VMEM((total_b, 128), jnp.float32),
            pltpu.VMEM((width // 128, total_b, 128), jnp.float32),
            pltpu.VMEM((width // 128, total_b, 128), jnp.float32),
            pltpu.VMEM((rows_c, total_b), jnp.float32),
            pltpu.VMEM((rows_c, total_b), jnp.float32),
            pltpu.VMEM((total_b, 2, rows_c, width), jnp.float32),
            pltpu.VMEM((2 * height, 2 * height), jnp.bfloat16),
            pltpu.VMEM((2 * height, 2 * height), jnp.bfloat16),
            pltpu.VMEM((each_b, 2, height, width), jnp.float32),
            pltpu.VMEM((2 * height, width), jnp.bfloat16),
            pltpu.VMEM((2 * height, width), jnp.bfloat16),
            pltpu.VMEM((2 * height, width), jnp.bfloat16),
            pltpu.VMEM((2 * height, width), jnp.bfloat16),
            pltpu.VMEM((2, n // 2, 2, rows, width), jnp.float32),
            pltpu.VMEM((2, n // 2, rows, width), jnp.float32),
            pltpu.VMEM((2, n - 1, rows, width), jnp.float32),
            pltpu.SemaphoreType.DMA((2,)),
            pltpu.SemaphoreType.DMA((each_b + 1,)),
            pltpu.SemaphoreType.DMA((each_b + 1,)),
            pltpu.SemaphoreType.DMA((width // 128, steps)),
            pltpu.SemaphoreType.DMA((width // 128, steps)),
        ],
        compiler_params=pltpu.CompilerParams(
            collective_id=0, has_side_effects=True, vmem_limit_bytes=56 * 2**20
        ),
    )(
        tiled, prop, first.reshape(1, -1), second.reshape(1, -1), third.reshape(1, -1), detune_steps
    )
    return jnp.transpose(result, (1, 0, 2))


def plain_density(phased, prop):
    def product(values, matrix):
        return jnp.einsum("ij,jba->iba", matrix, values, precision=lax.Precision.HIGHEST)

    def inner_rows(left, right):
        return lax.dot_general(
            left,
            right,
            (((0,), (0,)), ((), ())),
            precision=lax.Precision.HIGHEST,
            preferred_element_type=jnp.float32,
        )

    block = lax.all_to_all(phased, "cfg", split_axis=2, concat_axis=1, tiled=True)
    width = block.shape[3]
    real = (product(block[0], prop[0]) - product(block[1], prop[1])).reshape(-1, width)
    imag = (product(block[0], prop[1]) + product(block[1], prop[0])).reshape(-1, width)
    stacked = jnp.concatenate([real, imag], axis=0)
    crossed = inner_rows(imag, real)
    term = jnp.stack([inner_rows(stacked, stacked), crossed - crossed.T], axis=1)
    return lax.psum_scatter(term, "cfg", scatter_dimension=0, tiled=True)


def shards(n, amplitudes, prop_third, first, second, third, detune_steps):
    _, rows_c, total_b, width = amplitudes.shape
    height = prop_third.shape[1]
    fits = (
        n > 1
        and n & (n - 1) == 0
        and total_b % n == 0
        and total_b % 128 == 0
        and rows_c % 8 == 0
        and width % (8 * n) == 0
        and width % 512 == 0
        and height % 256 == 0
        and 256 % (2 * (width // n)) == 0
        and 12 * rows_c * total_b * width <= 2**24
    )
    if fits:
        return fused_density(
            amplitudes, prop_third, first, second, third, detune_steps, n
        )
    phased = apply_phases(amplitudes, factor_tables(first, second, third, detune_steps))
    return plain_density(phased, prop_third)


def solution(mesh):
    placed = (P("runs", "cfg", None, None), P(), P(), P(), P("cfg"), P("runs"))
    return jax.shard_map(
        functools.partial(shards, mesh.shape["cfg"]),
        mesh=mesh,
        in_specs=placed,
        out_specs=P(("runs", "cfg"), None, None),
        check_vma=False,
    )
```

```python
import functools
import jax
import jax.numpy as jnp
from jax import lax
from jax.experimental import pallas as pl
from jax.experimental.pallas import tpu as pltpu
from jax.sharding import PartitionSpec as P

angle_step = 0.2
pair_angle = 0.7
atom_count = 14
MESH = pl.DeviceIdType.MESH


def atom_bit(bitmasks, which):
    return (jnp.right_shift(bitmasks, which) & 1).astype(jnp.float32)


def occupation(bitmasks):
    total = jnp.zeros(bitmasks.shape, jnp.float32)
    for which in range(atom_count):
        total = total + atom_bit(bitmasks, which)
    return total


def factor_tables(first, second, third, detune_steps):
    scaled = detune_steps.astype(jnp.float32) * angle_step
    phase_first = scaled[0] * occupation(first)
    phase_second = scaled[1] * occupation(second)
    phase_third = scaled[2] * occupation(third)
    head, following = atom_bit(second, 0)[:, None], atom_bit(second, 1)[:, None]
    near, last = atom_bit(second, 12)[None, :], atom_bit(second, 13)[None, :]
    angle_ba = (
        phase_second[:, None]
        + phase_first[None, :]
        + pair_angle * (atom_bit(first, 12)[None, :] * head + atom_bit(first, 13)[None, :] * following)
    )
    allowed_ba = 1.0 - atom_bit(first, 13)[None, :] * head
    angle_cb = phase_third[:, None] + pair_angle * (
        near * atom_bit(third, 0)[:, None] + last * atom_bit(third, 1)[:, None]
    )
    allowed_cb = 1.0 - last * atom_bit(third, 0)[:, None]
    return lax.optimization_barrier(
        (
            allowed_ba * jnp.cos(angle_ba),
            allowed_ba * jnp.sin(angle_ba),
            allowed_cb * jnp.cos(angle_cb),
            allowed_cb * jnp.sin(angle_cb),
        )
    )


def apply_phases(amplitudes, tables):
    cos_ba, sin_ba, cos_cb, sin_cb = tables
    cos_cb, sin_cb = cos_cb[:, :, None], sin_cb[:, :, None]
    cosine = cos_ba[None] * cos_cb - sin_ba[None] * sin_cb
    sine = sin_ba[None] * cos_cb + cos_ba[None] * sin_cb
    return jnp.stack(
        [
            amplitudes[0] * cosine + amplitudes[1] * sine,
            amplitudes[1] * cosine - amplitudes[0] * sine,
        ]
    )


def split(values):
    high = values.astype(jnp.bfloat16)
    return high, (values - high.astype(jnp.float32)).astype(jnp.bfloat16)


def dot3(left, right, dims):
    def one(a, b):
        return lax.dot_general(a, b, (dims, ((), ())), preferred_element_type=jnp.float32)

    return one(left[0], right[0]) + (one(left[0], right[1]) + one(left[1], right[0]))


def column(row):
    size = row.shape[1]
    at = lax.broadcasted_iota(jnp.int32, (size, size), 0)
    across = lax.broadcasted_iota(jnp.int32, (size, size), 1)
    picked = jnp.where(at == across, row.astype(jnp.float32), 0.0)
    return jnp.sum(picked, axis=1, keepdims=True)


def part_order(part, steps):
    order = list(range(steps))
    if steps > 4:
        turned = [(1, 2, 3), (2, 1, 3), (3, 1, 2), (3, 2, 1)][part % 4]
        order[1:4] = turned
    return order


def density_kernel(
    n, amp_hbm, prop_hbm, first_ref, second_ref, third_ref, detune_ref, out_ref,
    amp, prop, second_col, cos_ba, sin_ba, cos_cb, sin_cb, outgoing, ah_ref, al_ref,
    recv, xh, xl, vh, vl, total, kept, landing,
    load_sem, send_sem, recv_sem, half_send, half_recv,
):
    steps = half_send.shape[1]
    me = lax.axis_index("cfg")
    total_b, _, rows_c, width = outgoing.shape
    each_b = total_b // n
    height = recv.shape[2]
    rows = out_ref.shape[1]

    load_amp = pltpu.make_async_copy(amp_hbm, amp, load_sem.at[0])
    load_prop = pltpu.make_async_copy(prop_hbm, prop, load_sem.at[1])
    load_amp.start()
    load_prop.start()

    barrier = pltpu.get_barrier_semaphore()

    def greet(s, carry):
        pl.semaphore_signal(
            barrier, inc=1, device_id={"cfg": lax.rem(me + s, n)}, device_id_type=MESH
        )
        return carry

    lax.fori_loop(1, n, greet, 0)

    def scaled(which):
        return detune_ref[which].astype(jnp.float32) * angle_step

    first, second = first_ref[...], second_ref[...]
    third = column(third_ref[...]).astype(jnp.int32)
    near, last = atom_bit(second, 12), atom_bit(second, 13)
    angle_cb = scaled(2) * occupation(third) + pair_angle * (
        near * atom_bit(third, 0) + last * atom_bit(third, 1)
    )
    allowed_cb = 1.0 - last * atom_bit(third, 0)
    cos_cb[...] = allowed_cb * jnp.cos(angle_cb)
    sin_cb[...] = allowed_cb * jnp.sin(angle_cb)
    second_col[...] = jnp.broadcast_to(column(second), second_col.shape)
    phase_first = scaled(0) * occupation(first)
    near_first, last_first = atom_bit(first, 12), atom_bit(first, 13)
    step_second = scaled(1)

    def table_rows(i, carry):
        at = pl.ds(pl.multiple_of(i * 8, 8), 8)
        mask = second_col[at, :][:, :1].astype(jnp.int32)
        head, following = atom_bit(mask, 0), atom_bit(mask, 1)
        angle = (
            step_second * occupation(mask)
            + phase_first
            + pair_angle * (near_first * head + last_first * following)
        )
        allowed = 1.0 - last_first * head
        cosine, sine = allowed * jnp.cos(angle), allowed * jnp.sin(angle)
        for k in range(width // 128):
            cos_ba[k, at, :] = cosine[:, k * 128 : (k + 1) * 128]
            sin_ba[k, at, :] = sine[:, k * 128 : (k + 1) * 128]
        return carry

    lax.fori_loop(0, total_b // 8, table_rows, 0)

    lane = lax.broadcasted_iota(jnp.int32, (rows_c, total_b), 1)
    columns = width // 128
    stride = total_b * columns

    def produce(b):
        here = lane == b
        cos_c = jnp.sum(jnp.where(here, cos_cb[...], 0.0), axis=1, keepdims=True)
        sin_c = jnp.sum(jnp.where(here, sin_cb[...], 0.0), axis=1, keepdims=True)
        for k in range(columns):
            lanes = slice(k * 128, (k + 1) * 128)
            start = ((b // 8) * columns + k) * 8 + lax.rem(b, 8)
            real = amp[0, pl.ds(start, rows_c, stride=stride), :]
            imag = amp[1, pl.ds(start, rows_c, stride=stride), :]
            cos_b = cos_ba[k, pl.ds(b, 1), :]
            sin_b = sin_ba[k, pl.ds(b, 1), :]
            cosine = cos_b * cos_c - sin_b * sin_c
            sine = sin_b * cos_c + cos_b * sin_c
            outgoing[b, 0, :, lanes] = real * cosine + imag * sine
            outgoing[b, 1, :, lanes] = imag * cosine - real * sine

    def place(j, lanes):
        return recv.at[j, :, pl.ds(pl.multiple_of(me * rows_c, rows_c), rows_c), lanes]

    def partner(i):
        k, odd = i // 2, lax.rem(i, 2)
        turn = lax.rem(k, 2)
        far = n // 2 + ((k + 1) // 2) * (1 - 2 * turn)
        near = (1 - turn) * (n - 1 - k // 2) + turn * ((k + 1) // 2)
        return lax.rem(me + (1 - odd) * far + odd * near, n)

    def send(i, j, lanes, sem):
        peer = partner(i)
        pltpu.make_async_remote_copy(
            src_ref=outgoing.at[peer * each_b + j, :, :, lanes],
            dst_ref=place(j, lanes),
            send_sem=send_sem.at[sem],
            recv_sem=recv_sem.at[sem],
            device_id={"cfg": peer},
            device_id_type=MESH,
        ).start()

    def keep(j, lanes, sem):
        pltpu.make_async_copy(
            outgoing.at[me * each_b + j, :, :, lanes], place(j, lanes), recv_sem.at[sem]
        ).start()

    everything = pl.ds(0, width)
    near_half, far_half = pl.ds(0, width // 2), pl.ds(width // 2, width // 2)

    load_amp.wait()
    pl.semaphore_wait(barrier, n - 1)

    def produce_all(j, lanes, sem):
        produce(me * each_b + j)
        produce(partner(jnp.int32(0)) * each_b + j)

        def next_pair(i, inner):
            produce(partner(i) * each_b + j)
            send(i - 1, j, lanes, sem)
            return inner

        lax.fori_loop(1, n - 1, next_pair, 0)
        keep(j, lanes, sem)
        send(jnp.int32(n - 2), j, lanes, sem)

    def send_all(j, carry):
        produce_all(j, everything, j)
        return carry

    final = each_b - 1
    lax.fori_loop(0, final, send_all, 0)
    produce_all(final, near_half, final)

    def send_rest(i, carry):
        send(i, final, far_half, final + 1)
        return carry

    lax.fori_loop(0, n - 1, send_rest, 0)
    keep(final, far_half, final + 1)
    load_prop.wait()

    def split_prop(i, carry):
        at = pl.ds(pl.multiple_of(i * 64, 64), 64)
        below = pl.ds(pl.multiple_of(height + i * 64, 64), 64)
        high, low = split(prop[0, at, :])
        ah_ref[at, :height] = high
        al_ref[at, :height] = low
        ah_ref[below, height:] = high
        al_ref[below, height:] = low
        high, low = split(prop[1, at, :])
        ah_ref[at, height:] = -high
        al_ref[at, height:] = -low
        ah_ref[below, :height] = high
        al_ref[below, :height] = low
        return carry

    lax.fori_loop(0, height // 64, split_prop, 0)
    total[...] = jnp.zeros_like(total)

    def arrived(b, lanes, sem):
        pltpu.make_async_copy(
            recv.at[b, :, :, lanes], recv.at[b, :, :, lanes], recv_sem.at[sem]
        ).wait()

    tile = 256

    def propagate(b, lanes):
        for part in range(2):
            def split_rows(t, inner):
                at = pl.ds(pl.multiple_of(t * 64, 64), 64)
                to = pl.ds(pl.multiple_of(part * height + t * 64, 64), 64)
                high, low = split(recv[b, part, at, lanes])
                xh[to, lanes] = high
                xl[to, lanes] = low
                return inner

            lax.fori_loop(0, height // 64, split_rows, 0)

        def evolve(t, inner):
            at = pl.ds(pl.multiple_of(t * tile, tile), tile)
            value = dot3(
                (ah_ref[at, :], al_ref[at, :]), (xh[:, lanes], xl[:, lanes]), ((1,), (0,))
            )
            high, low = split(value)
            vh[at, lanes] = high
            vl[at, lanes] = low
            return inner

        lax.fori_loop(0, 2 * height // tile, evolve, 0)

    def accumulate(left, right):
        def pieces(lanes):
            return (
                (vh[:height, lanes], vl[:height, lanes]),
                (vh[height:, lanes], vl[height:, lanes]),
            )

        real, imag = pieces(right)
        dims = ((0,), (0,))
        for at in range(left.start, left.stop, tile):
            real_t, imag_t = pieces(slice(at, at + tile))
            to = slice(at // (2 * rows), (at + tile) // (2 * rows))
            shape = (tile // (2 * rows), 2, rows, right.stop - right.start)
            term_real = dot3(real_t, real, dims) + dot3(imag_t, imag, dims)
            total[0, to, :, :, right] += term_real.reshape(shape)
            term_imag = dot3(imag_t, real, dims) - dot3(real_t, imag, dims)
            total[1, to, :, :, right] += term_imag.reshape(shape)

    middle = width // 2
    full, low_half, high_half = slice(0, width), slice(0, middle), slice(middle, width)

    def work(b, carry):
        arrived(b, everything, b)
        propagate(b, full)
        accumulate(full, full)
        return carry

    lax.fori_loop(0, final, work, 0)
    arrived(final, near_half, final)
    propagate(final, low_half)
    accumulate(low_half, low_half)
    arrived(final, far_half, final + 1)
    propagate(final, high_half)

    parts = width // 128
    orders = [part_order(p, steps) for p in range(parts)]
    offsets = [0] * parts

    def bit_of(index, which):
        return lax.rem(index // (2 ** which), 2)

    def halve(p, t):
        half = n >> (t + 1)
        which = orders[p][t]
        bit = bit_of(me, which)
        lanes = pl.ds(p * 128, 128)
        if t == 0:
            src = total.at[:, :, 1 - bit, :, lanes]
        else:
            src = kept.at[:, pl.ds(offsets[p] + (1 - bit) * half, half), :, lanes]
            offsets[p] = offsets[p] + bit * half
        copy = pltpu.make_async_remote_copy(
            src_ref=src,
            dst_ref=landing.at[:, pl.ds(n - 2 * half, half), :, lanes],
            send_sem=half_send.at[p, t],
            recv_sem=half_recv.at[p, t],
            device_id={"cfg": me + (1 - 2 * bit) * (2 ** which)},
            device_id_type=MESH,
        )
        copy.start()
        return copy

    def add(p, t):
        half = n >> (t + 1)
        lanes = slice(p * 128, (p + 1) * 128)
        if t == 0:
            core = bit_of(me, 0)

            def add_first(i, carry):
                where = 0
                for which in orders[p][1:]:
                    where = where * 2 + bit_of(i, which - 1)
                kept[:, where, :, lanes] = total[:, i, core, :, lanes] + landing[:, i, :, lanes]
                return carry

            lax.fori_loop(0, half, add_first, 0)
        else:
            first = n - 2 * half
            at = pl.ds(offsets[p], half)
            kept[:, at, :, lanes] += landing[:, first : first + half, :, lanes]

    flying = {}
    accumulate(full, high_half)
    for p in range(parts // 2, parts):
        flying[p] = halve(p, 0)
    accumulate(high_half, low_half)
    for p in range(parts // 2):
        flying[p] = halve(p, 0)
    for t in range(steps):
        for p in list(flying):
            flying[p].wait()
            add(p, t)
            if t + 1 < steps:
                flying[p] = halve(p, t + 1)
            else:
                lanes = slice(p * 128, (p + 1) * 128)
                out_ref[:, :, lanes] = kept[:, offsets[p], :, lanes]

    for j, lanes in enumerate([everything] * final + [near_half, far_half]):
        sent = outgoing.at[pl.ds(0, n - 1), :, :, lanes]
        pltpu.make_async_copy(sent, sent, send_sem.at[j]).wait()


def fused_density(amplitudes, prop, first, second, third, detune_steps, n):
    _, rows_c, total_b, width = amplitudes.shape
    height = prop.shape[1]
    each_b = total_b // n
    rows = width // n
    steps = n.bit_length() - 1
    tiled = amplitudes.reshape(2, rows_c, total_b // 8, 8, width // 128, 128)
    tiled = jnp.transpose(tiled, (0, 1, 2, 4, 3, 5)).reshape(2, -1, 128)
    vmem = pl.BlockSpec(memory_space=pltpu.VMEM)
    anywhere = pl.BlockSpec(memory_space=pl.ANY)
    result = pl.pallas_call(
        functools.partial(density_kernel, n),
        out_shape=jax.ShapeDtypeStruct((2, rows, width), jnp.float32),
        in_specs=[anywhere, anywhere, vmem, vmem, vmem, pl.BlockSpec(memory_space=pltpu.SMEM)],
        out_specs=vmem,
        scratch_shapes=[
            pltpu.VMEM(tiled.shape, jnp.float32),
            pltpu.VMEM(prop.shape, jnp.float32),
            pltpu.VMEM((total_b, 128), jnp.float32),
            pltpu.VMEM((width // 128, total_b, 128), jnp.float32),
            pltpu.VMEM((width // 128, total_b, 128), jnp.float32),
            pltpu.VMEM((rows_c, total_b), jnp.float32),
            pltpu.VMEM((rows_c, total_b), jnp.float32),
            pltpu.VMEM((total_b, 2, rows_c, width), jnp.float32),
            pltpu.VMEM((2 * height, 2 * height), jnp.bfloat16),
            pltpu.VMEM((2 * height, 2 * height), jnp.bfloat16),
            pltpu.VMEM((each_b, 2, height, width), jnp.float32),
            pltpu.VMEM((2 * height, width), jnp.bfloat16),
            pltpu.VMEM((2 * height, width), jnp.bfloat16),
            pltpu.VMEM((2 * height, width), jnp.bfloat16),
            pltpu.VMEM((2 * height, width), jnp.bfloat16),
            pltpu.VMEM((2, n // 2, 2, rows, width), jnp.float32),
            pltpu.VMEM((2, n // 2, rows, width), jnp.float32),
            pltpu.VMEM((2, n - 1, rows, width), jnp.float32),
            pltpu.SemaphoreType.DMA((2,)),
            pltpu.SemaphoreType.DMA((each_b + 1,)),
            pltpu.SemaphoreType.DMA((each_b + 1,)),
            pltpu.SemaphoreType.DMA((width // 128, steps)),
            pltpu.SemaphoreType.DMA((width // 128, steps)),
        ],
        compiler_params=pltpu.CompilerParams(
            collective_id=0, has_side_effects=True, vmem_limit_bytes=56 * 2**20
        ),
    )(
        tiled, prop, first.reshape(1, -1), second.reshape(1, -1), third.reshape(1, -1), detune_steps
    )
    return jnp.transpose(result, (1, 0, 2))


def plain_density(phased, prop):
    def product(values, matrix):
        return jnp.einsum("ij,jba->iba", matrix, values, precision=lax.Precision.HIGHEST)

    def inner_rows(left, right):
        return lax.dot_general(
            left,
            right,
            (((0,), (0,)), ((), ())),
            precision=lax.Precision.HIGHEST,
            preferred_element_type=jnp.float32,
        )

    block = lax.all_to_all(phased, "cfg", split_axis=2, concat_axis=1, tiled=True)
    width = block.shape[3]
    real = (product(block[0], prop[0]) - product(block[1], prop[1])).reshape(-1, width)
    imag = (product(block[0], prop[1]) + product(block[1], prop[0])).reshape(-1, width)
    stacked = jnp.concatenate([real, imag], axis=0)
    crossed = inner_rows(imag, real)
    term = jnp.stack([inner_rows(stacked, stacked), crossed - crossed.T], axis=1)
    return lax.psum_scatter(term, "cfg", scatter_dimension=0, tiled=True)


def shards(n, amplitudes, prop_third, first, second, third, detune_steps):
    _, rows_c, total_b, width = amplitudes.shape
    height = prop_third.shape[1]
    fits = (
        n > 1
        and n & (n - 1) == 0
        and total_b % n == 0
        and total_b % 128 == 0
        and rows_c % 8 == 0
        and width % (8 * n) == 0
        and width % 512 == 0
        and height % 256 == 0
        and 256 % (2 * (width // n)) == 0
        and 12 * rows_c * total_b * width <= 2**24
    )
    if fits:
        return fused_density(
            amplitudes, prop_third, first, second, third, detune_steps, n
        )
    phased = apply_phases(amplitudes, factor_tables(first, second, third, detune_steps))
    return plain_density(phased, prop_third)


def solution(mesh):
    placed = (P("runs", "cfg", None, None), P(), P(), P(), P("cfg"), P("runs"))
    return jax.shard_map(
        functools.partial(shards, mesh.shape["cfg"]),
        mesh=mesh,
        in_specs=placed,
        out_specs=P(("runs", "cfg"), None, None),
        check_vma=False,
    )
```
